32 devices in a mesh: groups: 2 (over y), pb: 16 (over z, x, core).
Axes of the slice: x: 2, y: 2, z: 4, core: 2. Of those that a mesh axis runs over, the one named last changes fastest.
Arguments:
- fields: float32 [32, 16, 512], P(('groups', 'pb')), parts along dimension 0, may hold values from -6 to 6
- field_shift: float32 [16, 512], replicated, may hold values from -1 to 1
- cholesky: bfloat16 [512, 1024, 1024], P(None, 'pb'), may hold values from -0.015625 to 0.015625
- onebody: float32 [16, 64], replicated, may hold values from -0.5 to 0.5
- walkers: bfloat16 [32, 1024, 256], P(('groups', 'pb')), parts along dimension 0, may hold values from -6 to 6
Outputs:
- propagated: bfloat16 [32, 1024, 256], P(('groups', 'pb')), parts along dimension 0
The draws below stay inside these ranges and needn't reach their ends.
There are 2 independent parts, one for each index of `groups`. The reference program is written for one: setup_inputs(seed, part) draws one part's arguments, and reference() takes and returns one part's arrays. A program takes and returns all parts, laid end to end along the dimension named above; an argument that names none is the same for every part. Nothing has to cross between parts.
All inputs are finite; a program needn't handle non-finite values.
Results may differ from the reference program's by a relative error of at most 0.0089.
Values may be sent and summed in bfloat16 or wider, within the bound.
A program may use at most 192 MiB of HBM per device.

```python
import jax
import jax.numpy as jnp
from jax import lax

NK = 16
NORB = 64
NCHOL = 512
COLS = 256
TERMS = 6
WALKERS = 16


def level_of(key, shape, shards, smallest, largest):
    factor_of = 1.0
    for position, shards_of in shards:
        steps = jax.random.uniform(jax.random.fold_in(jax.random.fold_in(key, 6), position), (shards_of,), jnp.float32, smallest / len(shards), largest / len(shards))
        factor_of = factor_of * jnp.repeat(jnp.exp(steps), shape[position] // shards_of).reshape((-1,) + (1,) * (len(shape) - 1 - position))
    return factor_of


def gaussian(stream_key, extent, width, bound, shards=(), dtype=jnp.bfloat16):
    level = level_of(stream_key, extent, shards, -0.22, 0.18) if shards else 1.0
    entries = jax.random.normal(stream_key, extent, jnp.float32) * width * level
    return jnp.minimum(jnp.maximum(entries, -bound), bound).astype(dtype)


def setup_inputs(seed: int = 0, part: int = 0) -> dict:
    keys = jax.random.split(jax.random.key(seed), 6)
    part_splits = jax.random.split(jax.random.fold_in(keys[5], part), 6)
    return {
        "fields": gaussian(part_splits[0], (WALKERS, NK, NCHOL), 1.0, 6.0, ((0, 16),), jnp.float32),
        "field_shift": jnp.clip(jax.random.uniform(keys[1], (NK, NCHOL), jnp.float32, -1.0, 1.0), -1.0, 1.0),
        "cholesky": gaussian(keys[2], (NCHOL, NK * NORB, NK * NORB), (NCHOL * NK * NORB // 4) ** -0.5, 0.015625, ((1, 16),)),
        "onebody": jnp.clip(jax.random.uniform(keys[3], (NK, NORB), jnp.float32, -0.5, 0.5), -0.5, 0.5),
        "walkers": gaussian(part_splits[4], (WALKERS, NK * NORB, COLS), 1.0, 6.0, ((0, 16),)),
    }


def taylor(potential, determinant, onebody):
    term = determinant
    total = determinant.astype(jnp.float32)
    for order in range(1, TERMS):
        rolled = jnp.stack([jnp.roll(term, transfer, axis=0) for transfer in range(NK)], axis=1)
        rolled = rolled.reshape(NK, NK * NORB, COLS)
        product = jnp.einsum("kaj,kjc->kac", potential.astype(jnp.float32), rolled.astype(jnp.float32), precision=lax.Precision.HIGHEST)
        product = product + onebody[:, :, None] * term.astype(jnp.float32)
        term = (product * (-1.0 / order)).astype(jnp.bfloat16)
        total = total + term.astype(jnp.float32)
    return total.astype(jnp.bfloat16)


def reference(fields, field_shift, cholesky, onebody, walkers):
    count = fields.shape[0]
    shifted = (fields + field_shift[None]).astype(jnp.bfloat16)
    blocks = []
    for transfer in range(NK):
        slab = cholesky[:, transfer * NORB:(transfer + 1) * NORB, :].reshape(NCHOL, NORB * NK * NORB)
        blocks.append(jnp.dot(shifted[:, transfer, :], slab, preferred_element_type=jnp.float32).astype(jnp.bfloat16))
    potential_all = jnp.stack(blocks, axis=1).reshape(count, NK, NORB, NK, NORB)

    def propagate(pair):
        blocks_one, determinant = pair
        potential = blocks_one.transpose(2, 1, 0, 3).reshape(NK, NORB, NK * NORB)
        result = taylor(potential, determinant.reshape(NK, NORB, COLS), onebody)
        return result.reshape(NK * NORB, COLS)

    return lax.map(propagate, (potential_all, walkers))
```

```python
import functools

import jax
import jax.numpy as jnp
from jax import lax
from jax.experimental import pallas as pl
from jax.experimental.pallas import tpu as pltpu
from jax.sharding import PartitionSpec as P

TERMS = 6
MESH = pl.DeviceIdType.MESH
ROWS = 16
SLOTS = 8
SPLITS = 4
PIECE = 2048
STEP = 256
AHEAD = 3
VMEM_EXCHANGE = 58 * 1024 * 1024
VMEM_SERIES = 16 * 1024 * 1024


def plain(fields, field_shift, cholesky, onebody, walkers):
    devices = lax.axis_size("pb")
    local_walkers = fields.shape[0]
    kpoints = field_shift.shape[0]
    orbitals = onebody.shape[1]
    vectors = field_shift.shape[1]
    rows_here = cholesky.shape[1]
    per_transfer = orbitals // rows_here
    slab = cholesky.reshape(vectors, rows_here * kpoints * orbitals)
    shifted = (fields + field_shift[None]).astype(jnp.bfloat16)
    outgoing = jnp.repeat(shifted, per_transfer, axis=1)
    arrived = lax.all_to_all(outgoing, "pb", split_axis=1, concat_axis=0, tiled=True)
    partial_blocks = jnp.dot(arrived[:, 0, :], slab, preferred_element_type=jnp.float32).astype(
        jnp.bfloat16
    )
    outgoing_blocks = partial_blocks.reshape(devices, local_walkers, rows_here * kpoints * orbitals)
    relayed = lax.all_to_all(outgoing_blocks, "pb", split_axis=0, concat_axis=0, tiled=True)
    relayed = relayed.reshape(kpoints, per_transfer, local_walkers, rows_here, kpoints, orbitals)
    potential = relayed.transpose(2, 4, 1, 3, 0, 5).reshape(
        local_walkers, kpoints, orbitals, kpoints, orbitals
    )
    turned = jnp.flip(potential, axis=3)
    permuted = jnp.stack(
        [jnp.roll(turned[:, k], k + 1, axis=2) for k in range(kpoints)], axis=1
    )
    permuted = permuted.reshape(local_walkers, kpoints * orbitals, kpoints * orbitals)
    diagonal_term = onebody.reshape(kpoints * orbitals)[None, :, None]
    term = walkers
    total = term.astype(jnp.float32)
    for order in range(1, TERMS):
        product = jnp.einsum("wij,wjc->wic", permuted, term, preferred_element_type=jnp.float32)
        product = product + diagonal_term * term.astype(jnp.float32)
        term = (product * (-1.0 / order)).astype(jnp.bfloat16)
        total = total + term.astype(jnp.float32)
    return total.astype(jnp.bfloat16)


def exchange(
    n, nk, norb, fields_hbm, shift_hbm, onebody_hbm, chol_hbm, walker_hbm, matrix, first,
    fields, shift, onebody, fields_out, fields_in, lines, spread, left, buf, blocks_out, blocks_in, rows_in,
    pairs, walker, fsem, fsend, frecv, csem, bsend, brecv, wsem,
):
    me = lax.axis_index("pb")
    nchol = chol_hbm.shape[0]
    width = chol_hbm.shape[2]
    cols = buf.shape[3]
    slots = buf.shape[0]
    row_blocks = norb // ROWS
    chunks = row_blocks * (width // cols)
    k_here = cols // norb
    group = 128
    wide = group * ROWS
    half, quarter = n // 2, n // 4
    mine = me // half
    outer = jnp.where((me // quarter) % 3 == 0, 1, 0)
    places = [r for r in range(n) if r != half]
    parts = [range(0, quarter), range(quarter, half), range(half, n)]

    def peer_of(r):
        if r < half:
            row = 2 - mine if r < quarter else 3 * (1 - mine)
            return row * quarter + lax.rem(me + r, quarter)
        return mine * half + lax.rem(me + r, half)

    def tensor_copy(c, slot):
        h, i = c // row_blocks, c % row_blocks
        return pltpu.make_async_copy(
            chol_hbm.at[:, pl.ds(pl.multiple_of(i * ROWS, ROWS), ROWS), pl.ds(pl.multiple_of(h * cols, cols), cols)],
            buf.at[slot],
            csem.at[slot],
        )

    barrier = pltpu.get_barrier_semaphore()
    for r in places:
        pl.semaphore_signal(barrier, inc=1, device_id={"pb": peer_of(r)}, device_id_type=MESH)
    small = [
        pltpu.make_async_copy(fields_hbm, fields, fsem.at[0]),
        pltpu.make_async_copy(shift_hbm, shift, fsem.at[1]),
        pltpu.make_async_copy(onebody_hbm, onebody, fsem.at[2]),
    ]
    for copy in small:
        copy.start()
    for c in range(min(slots, chunks)):
        tensor_copy(c, c).start()
    walker_copy = pltpu.make_async_copy(walker_hbm, walker, wsem)
    walker_copy.start()
    small[0].wait()
    for q in range(nk):
        fields_out[q] = fields[q : q + 1, :]
    fields_in[me] = fields_out[me]
    spread[...] = (
        lax.broadcasted_iota(jnp.int32, (group, wide), 1) // ROWS
        == lax.broadcasted_iota(jnp.int32, (group, wide), 0)
    ).astype(jnp.float32).astype(jnp.bfloat16)
    for copy in small[1:]:
        copy.wait()
    for k in range(nk):
        pairs[k // 2, :, k % 2 * norb : (k % 2 + 1) * norb] = onebody[k : k + 1, :]
    pl.semaphore_wait(barrier, n - 1)

    def field_copy(r):
        peer = peer_of(r)
        return pltpu.make_async_remote_copy(
            src_ref=fields_out.at[peer], dst_ref=fields_in.at[me], send_sem=fsend,
            recv_sem=frecv.at[outer if r < half else 2], device_id={"pb": peer}, device_id_type=MESH,
        )

    for r in places:
        field_copy(r).start()

    def fields_of(count, sem):
        some = pl.ds(0, count)
        return pltpu.make_async_remote_copy(
            src_ref=fields_out.at[some], dst_ref=fields_in.at[some], send_sem=fsend,
            recv_sem=frecv.at[sem], device_id={"pb": peer_of(0)}, device_id_type=MESH,
        )

    mask = (
        lax.broadcasted_iota(jnp.int32, (ROWS, wide), 1) % ROWS
        == lax.broadcasted_iota(jnp.int32, (ROWS, wide), 0)
    )

    def block_copy(c, r):
        peer = peer_of(r)
        return pltpu.make_async_remote_copy(
            src_ref=blocks_out.at[c, r], dst_ref=blocks_in.at[c, me], send_sem=bsend,
            recv_sem=brecv.at[c], device_id={"pb": peer}, device_id_type=MESH,
        )

    vectors_piece = PIECE // ROWS

    def build(part):
        lo, hi = part[0], part[-1] + 1
        base = lo // 8 * 8
        for r in part:
            lines[r : r + 1, :] = fields_in[peer_of(r)]
        shifted = (lines[base : base + 8, :] + shift[pl.ds(me, 1), :]).astype(jnp.bfloat16)
        for b in range(nchol // group):
            spreaded = jnp.dot(
                shifted[:, b * group : (b + 1) * group], spread[...],
                preferred_element_type=jnp.float32,
            )
            for r in range(lo, hi):
                line = jnp.broadcast_to(spreaded[r - base : r - base + 1, :], (ROWS, wide))
                left[r * ROWS : (r + 1) * ROWS, b * wide : (b + 1) * wide] = jnp.where(
                    mask, line, 0.0
                ).astype(jnp.bfloat16)

    def multiply(c, lo, hi):
        slot = lax.rem(c, slots)
        total = None
        for p in range(nchol // vectors_piece):
            right = buf[slot, p * vectors_piece : (p + 1) * vectors_piece].reshape(PIECE, cols)
            product = jnp.dot(
                left[lo * ROWS : hi * ROWS, p * PIECE : (p + 1) * PIECE],
                right, preferred_element_type=jnp.float32,
            )
            total = product if total is None else total + product
        blocks_out[c, lo:hi] = total.astype(jnp.bfloat16).reshape(hi - lo, ROWS, cols)

    def send(c, part):
        for r in part:
            if r != half:
                block_copy(c, r).start()

    def far(c, carry):
        tensor_copy(c, lax.rem(c, slots)).wait()
        multiply(c, 0, half)
        send(c, [*parts[1], *parts[0]])
        return carry

    def near(c, carry):
        multiply(c, half, n)
        send(c, parts[2])
        blocks_in[c, me] = blocks_out[c, half]
        if slots < chunks:
            tensor_copy(c + slots, lax.rem(c, slots)).start()
        return carry

    def both(c, carry):
        slot = lax.rem(c, slots)
        tensor_copy(c, slot).wait()
        multiply(c, 0, n)
        send(c, [*parts[1], *parts[0], *parts[2]])
        blocks_in[c, me] = blocks_out[c, half]

        @pl.when(c + slots < chunks)
        def _():
            tensor_copy(c + slots, slot).start()

        return carry

    lines[...] = jnp.zeros_like(lines)
    fields_of(quarter, 0).wait_recv()
    build(parts[0])
    tensor_copy(0, 0).wait()
    multiply(0, 0, quarter)
    send(0, parts[0])
    fields_of(quarter, 1).wait_recv()
    build(parts[1])
    multiply(0, quarter, half)
    send(0, parts[1])
    lax.fori_loop(1, AHEAD, far, 0)
    fields_of(half - 1, 2).wait_recv()
    build(parts[2])
    lax.fori_loop(0, AHEAD, near, 0)
    lax.fori_loop(AHEAD, chunks, both, 0)
    walker_copy.wait()
    others = pl.ds(0, n - 1)
    lane = lax.broadcasted_iota(jnp.int32, (ROWS, 128), 1)
    row = lax.broadcasted_iota(jnp.int32, (ROWS, 128), 0)

    def assemble(c, carry):
        h, i = c // row_blocks, c % row_blocks
        pltpu.make_async_remote_copy(
            src_ref=blocks_out.at[c, others], dst_ref=blocks_in.at[c, others], send_sem=bsend,
            recv_sem=brecv.at[c], device_id={"pb": peer_of(0)}, device_id_type=MESH,
        ).wait_recv()
        for kk in range(k_here):
            k = h * k_here + kk
            start = kk // 2 * 128
            off = kk % 2 * norb
            rows = pl.ds(pl.multiple_of(k * norb + i * ROWS, ROWS), ROWS)
            here = slice(kk * ROWS, (kk + 1) * ROWS)
            for pair in range(nk // 2):
                one = blocks_in[c, lax.rem(k - 2 * pair + nk, nk), :, start : start + 128]
                two = blocks_in[c, lax.rem(k - 2 * pair - 1 + nk, nk), :, start : start + 128]
                rows_in[here, pair * 128 : (pair + 1) * 128] = jnp.concatenate(
                    [one[:, off : off + norb], two[:, off : off + norb]], axis=1
                )
            place = pl.ds(pl.multiple_of(k // 2 * 128, 128), 128)
            extra = jnp.where(lane == row + (off + i * ROWS), jnp.broadcast_to(pairs[k // 2], (ROWS, 128)), 0.0)
            rows_in[here, place] = (rows_in[here, place].astype(jnp.float32) + extra).astype(jnp.bfloat16)
            matrix[rows, :] = rows_in[here, :]
        product = jnp.dot(rows_in[...], walker[...], preferred_element_type=jnp.float32)
        for kk in range(k_here):
            rows = pl.ds(pl.multiple_of((h * k_here + kk) * norb + i * ROWS, ROWS), ROWS)
            first[rows, :] = (-product[kk * ROWS : (kk + 1) * ROWS]).astype(jnp.bfloat16)
        return carry

    lax.fori_loop(0, chunks, assemble, 0)
    fields_of(n - 1, 0).wait_send()
    pltpu.make_async_remote_copy(
        src_ref=blocks_out.at[:, others], dst_ref=blocks_in.at[:, others], send_sem=bsend,
        recv_sem=brecv.at[0], device_id={"pb": peer_of(0)}, device_id_type=MESH,
    ).wait_send()


def series(matrix, first, walker_hbm, out_hbm, walker, term_a, term_b, total, out, wsem, osem):
    size = matrix.shape[0]
    copy = pltpu.make_async_copy(walker_hbm, walker, wsem)
    copy.start()
    copies = []
    for number in range(2, TERMS):
        source = first if number == 2 else (term_a, term_b)[number % 2]
        target = (term_b, term_a)[number % 2]
        for r in range(0, size, STEP):
            rows = slice(r, r + STEP)
            product = jnp.dot(matrix[rows, :], source[...], preferred_element_type=jnp.float32)
            term = (product * (-1.0 / number)).astype(jnp.bfloat16)
            if number == 2:
                if r == 0:
                    copy.wait()
                before = walker[rows, :].astype(jnp.float32) + first[rows, :].astype(jnp.float32)
            else:
                before = total[rows, :]
            after = before + term.astype(jnp.float32)
            if number < TERMS - 1:
                target[rows, :] = term
                total[rows, :] = after
            else:
                out[rows, :] = after.astype(jnp.bfloat16)
                copies.append(pltpu.make_async_copy(out.at[rows, :], out_hbm.at[rows, :], osem.at[r // STEP]))
                copies[-1].start()
    for copy in copies:
        copy.wait()


def fused(fields, field_shift, cholesky, onebody, walkers):
    n = lax.axis_size("pb")
    nk, norb = onebody.shape
    nchol = cholesky.shape[0]
    width = cholesky.shape[2]
    cols = width // SPLITS
    chunks = norb // ROWS * SPLITS
    slots = min(SLOTS, chunks)
    size, columns = walkers.shape[1:]
    bf16, f32 = jnp.bfloat16, jnp.float32
    vmem = pl.BlockSpec(memory_space=pltpu.VMEM)
    hbm = pl.BlockSpec(memory_space=pl.ANY)
    walker = walkers.reshape(size, columns)
    matrix, first = pl.pallas_call(
        functools.partial(exchange, n, nk, norb),
        out_shape=(pltpu.VMEM((size, size), bf16), pltpu.VMEM((size, columns), bf16)),
        in_specs=[hbm] * 5,
        out_specs=(vmem, vmem),
        scratch_shapes=[
            pltpu.VMEM((nk, nchol), f32),
            pltpu.VMEM(field_shift.shape, f32),
            pltpu.VMEM((nk, norb), f32),
            pltpu.VMEM((nk, 1, nchol), f32),
            pltpu.VMEM((n, 1, nchol), f32),
            pltpu.VMEM((n, nchol), f32),
            pltpu.VMEM((128, 128 * ROWS), bf16),
            pltpu.VMEM((n * ROWS, nchol * ROWS), bf16),
            pltpu.VMEM((slots, nchol, ROWS, cols), bf16),
            pltpu.VMEM((chunks, n, ROWS, cols), bf16),
            pltpu.VMEM((chunks, n, ROWS, cols), bf16),
            pltpu.VMEM((cols // norb * ROWS, size), bf16),
            pltpu.VMEM((nk // 2, 1, 2 * norb), f32),
            pltpu.VMEM((size, columns), bf16),
            pltpu.SemaphoreType.DMA((3,)),
            pltpu.SemaphoreType.DMA,
            pltpu.SemaphoreType.DMA((3,)),
            pltpu.SemaphoreType.DMA((slots,)),
            pltpu.SemaphoreType.DMA,
            pltpu.SemaphoreType.DMA((chunks,)),
            pltpu.SemaphoreType.DMA,
        ],
        compiler_params=pltpu.CompilerParams(
            collective_id=0, has_side_effects=True, vmem_limit_bytes=VMEM_EXCHANGE
        ),
    )(fields.reshape(nk, nchol), field_shift, onebody, cholesky, walker)
    out = pl.pallas_call(
        series,
        out_shape=jax.ShapeDtypeStruct((size, columns), bf16),
        in_specs=[vmem, vmem, hbm],
        out_specs=hbm,
        scratch_shapes=[
            pltpu.VMEM((size, columns), bf16),
            pltpu.VMEM((size, columns), bf16),
            pltpu.VMEM((size, columns), bf16),
            pltpu.VMEM((size, columns), f32),
            pltpu.VMEM((size, columns), bf16),
            pltpu.SemaphoreType.DMA,
            pltpu.SemaphoreType.DMA((size // STEP,)),
        ],
        compiler_params=pltpu.CompilerParams(vmem_limit_bytes=VMEM_SERIES),
    )(matrix, first, walker)
    return out.reshape(walkers.shape)


def per_device(fields, field_shift, cholesky, onebody, walkers):
    n = lax.axis_size("pb")
    nk, norb = onebody.shape
    fits = (
        fields.shape[0] == 1 and n == nk and n % 4 == 0 and cholesky.shape[1] == norb and norb == 64
        and walkers.shape[2] % 128 == 0 and cholesky.shape[0] % 128 == 0
    )
    body = fused if fits else plain
    return body(fields, field_shift, cholesky, onebody, walkers)


def solution(mesh):
    return jax.shard_map(
        per_device,
        mesh=mesh,
        in_specs=(
            P(("groups", "pb"), None, None),
            P(),
            P(None, "pb", None),
            P(),
            P(("groups", "pb"), None, None),
        ),
        out_specs=P(("groups", "pb"), None, None),
        check_vma=False,
    )
```

```python
import functools

import jax
import jax.numpy as jnp
from jax import lax
from jax.experimental import pallas as pl
from jax.experimental.pallas import tpu as pltpu
from jax.sharding import PartitionSpec as P

TERMS = 6
MESH = pl.DeviceIdType.MESH
ROWS = 16
SLOTS = 8
SPLITS = 4
PIECE = 2048
STEP = 256
AHEAD = 3
FIRST = 3
BEHIND = 2
VMEM_EXCHANGE = 58 * 1024 * 1024
VMEM_SERIES = 16 * 1024 * 1024


def plain(fields, field_shift, cholesky, onebody, walkers):
    devices = lax.axis_size("pb")
    local_walkers = fields.shape[0]
    kpoints = field_shift.shape[0]
    orbitals = onebody.shape[1]
    vectors = field_shift.shape[1]
    rows_here = cholesky.shape[1]
    per_transfer = orbitals // rows_here
    slab = cholesky.reshape(vectors, rows_here * kpoints * orbitals)
    shifted = (fields + field_shift[None]).astype(jnp.bfloat16)
    outgoing = jnp.repeat(shifted, per_transfer, axis=1)
    arrived = lax.all_to_all(outgoing, "pb", split_axis=1, concat_axis=0, tiled=True)
    partial_blocks = jnp.dot(arrived[:, 0, :], slab, preferred_element_type=jnp.float32).astype(
        jnp.bfloat16
    )
    outgoing_blocks = partial_blocks.reshape(devices, local_walkers, rows_here * kpoints * orbitals)
    relayed = lax.all_to_all(outgoing_blocks, "pb", split_axis=0, concat_axis=0, tiled=True)
    relayed = relayed.reshape(kpoints, per_transfer, local_walkers, rows_here, kpoints, orbitals)
    potential = relayed.transpose(2, 4, 1, 3, 0, 5).reshape(
        local_walkers, kpoints, orbitals, kpoints, orbitals
    )
    turned = jnp.flip(potential, axis=3)
    permuted = jnp.stack(
        [jnp.roll(turned[:, k], k + 1, axis=2) for k in range(kpoints)], axis=1
    )
    permuted = permuted.reshape(local_walkers, kpoints * orbitals, kpoints * orbitals)
    diagonal_term = onebody.reshape(kpoints * orbitals)[None, :, None]
    term = walkers
    total = term.astype(jnp.float32)
    for order in range(1, TERMS):
        product = jnp.einsum("wij,wjc->wic", permuted, term, preferred_element_type=jnp.float32)
        product = product + diagonal_term * term.astype(jnp.float32)
        term = (product * (-1.0 / order)).astype(jnp.bfloat16)
        total = total + term.astype(jnp.float32)
    return total.astype(jnp.bfloat16)


def exchange(
    n, nk, norb, fields_hbm, shift_hbm, onebody_hbm, chol_hbm, walker_hbm, matrix, first,
    fields, shift, onebody, fields_out, fields_in, lines, spread, left, buf, blocks_out, blocks_in, rows_in,
    pairs, walker, fsem, fsend, frecv, csem, bsend, brecv, wsem, ready,
):
    me = lax.axis_index("pb")
    nchol = chol_hbm.shape[0]
    width = chol_hbm.shape[2]
    cols = buf.shape[3]
    slots = buf.shape[0]
    row_blocks = norb // ROWS
    chunks = row_blocks * (width // cols)
    reach = slots - AHEAD
    k_here = cols // norb
    group = 128
    wide = group * ROWS
    half, quarter = n // 2, n // 4
    mine = me // half
    places = [r for r in range(n) if r != half]

    def peer_of(r):
        if r < half:
            row = 2 - mine if r < quarter else 3 * (1 - mine)
            return row * quarter + lax.rem(me + r, quarter)
        return mine * half + lax.rem(me + r, half)

    def tensor_copy(c, slot):
        h, i = c // row_blocks, c % row_blocks
        return pltpu.make_async_copy(
            chol_hbm.at[:, pl.ds(pl.multiple_of(i * ROWS, ROWS), ROWS), pl.ds(pl.multiple_of(h * cols, cols), cols)],
            buf.at[slot],
            csem.at[slot],
        )

    def peer_at(r):
        far = jnp.where(r < quarter, 2 - mine, 3 * (1 - mine)) * quarter + lax.rem(me + r, quarter)
        return jnp.where(r < half, far, mine * half + lax.rem(me + r, half))

    def fetch(c):
        if c < chunks:
            tensor_copy(c, c % slots).start()

    barrier = pltpu.get_barrier_semaphore()
    for r in places:
        peer = peer_of(r)

        @pl.when(peer > me)
        def _():
            pl.semaphore_signal(barrier, inc=1, device_id={"pb": peer}, device_id_type=MESH)

    small = [
        pltpu.make_async_copy(fields_hbm, fields, fsem.at[0]),
        pltpu.make_async_copy(shift_hbm, shift, fsem.at[1]),
        pltpu.make_async_copy(onebody_hbm, onebody, fsem.at[2]),
    ]
    for copy in small:
        copy.start()
    for c in range(FIRST):
        fetch(c)
    walker_copy = pltpu.make_async_copy(walker_hbm, walker, wsem)
    walker_copy.start()
    small[0].wait()
    for q in range(nk):
        fields_out[q] = fields[q : q + 1, :]
    fields_in[me] = fields_out[me]
    spread[...] = (
        lax.broadcasted_iota(jnp.int32, (group, wide), 1) // ROWS
        == lax.broadcasted_iota(jnp.int32, (group, wide), 0)
    ).astype(jnp.float32).astype(jnp.bfloat16)
    for copy in small[1:]:
        copy.wait()
    for k in range(nk):
        pairs[k // 2, :, k % 2 * norb : (k % 2 + 1) * norb] = onebody[k : k + 1, :]

    kind = jnp.where((me // quarter) % 3 == 0, 1, 0)

    def field_copy(r):
        peer = peer_of(r)
        return pltpu.make_async_remote_copy(
            src_ref=fields_out.at[peer], dst_ref=fields_in.at[me], send_sem=fsend.at[0 if r < half else 1],
            recv_sem=frecv.at[kind if r < half else 2], device_id={"pb": peer}, device_id_type=MESH,
        )

    def fields_of(count, send, number):
        some = pl.ds(0, count)
        return pltpu.make_async_remote_copy(
            src_ref=fields_out.at[some], dst_ref=fields_in.at[some], send_sem=fsend.at[send],
            recv_sem=frecv.at[number], device_id={"pb": peer_of(0)}, device_id_type=MESH,
        )


    @pl.when(me > 0)
    def _():
        pl.semaphore_wait(barrier, me)

    late = (me // quarter) % 2

    @pl.when(mine == 1)
    def _():
        for r in [*range(quarter), *range(quarter, half)]:
            pl.semaphore_signal(ready.at[late], inc=1, device_id={"pb": peer_of(r)}, device_id_type=MESH)
        for r in range(half):
            field_copy(r).start()

    for r in range(half + 1, n):
        peer = peer_of(r)

        @pl.when(peer < me)
        def _():
            pl.semaphore_signal(ready.at[2], inc=1, device_id={"pb": peer}, device_id_type=MESH)

    @pl.when(mine == 0)
    def _():
        for part in range(2):
            pl.semaphore_wait(ready.at[part], quarter)
            for r in range(part * quarter, (part + 1) * quarter):
                field_copy(r).start()

    above = half - 1 - lax.rem(me, half)

    @pl.when(above > 0)
    def _():
        pl.semaphore_wait(ready.at[2], above)

    for r in range(half + 1, n):
        field_copy(r).start()
    for c in range(FIRST, reach):
        fetch(c)

    mask = (
        lax.broadcasted_iota(jnp.int32, (ROWS, wide), 1) % ROWS
        == lax.broadcasted_iota(jnp.int32, (ROWS, wide), 0)
    )

    def block_copy(c, r):
        peer = peer_of(r)
        return pltpu.make_async_remote_copy(
            src_ref=blocks_out.at[c, r], dst_ref=blocks_in.at[c, me], send_sem=bsend,
            recv_sem=brecv.at[c], device_id={"pb": peer}, device_id_type=MESH,
        )

    vectors_piece = PIECE // ROWS

    def build(fourth):
        for r in range(quarter):
            lines[r : r + 1, :] = fields_in[peer_at(fourth * quarter + r)]
        shifted = (lines[...] + shift[pl.ds(me, 1), :]).astype(jnp.bfloat16)
        for b in range(nchol // group):
            spreaded = jnp.dot(
                shifted[:, b * group : (b + 1) * group], spread[...],
                preferred_element_type=jnp.float32,
            )
            for r in range(quarter):
                line = jnp.broadcast_to(spreaded[r : r + 1, :], (ROWS, wide))
                start = (fourth % 2 * quarter + r) * ROWS
                left[fourth // 2, pl.ds(pl.multiple_of(start, ROWS), ROWS), b * wide : (b + 1) * wide] = jnp.where(
                    mask, line, 0.0
                ).astype(jnp.bfloat16)

    def multiply(c, slot, part, start, count):
        rows = pl.ds(pl.multiple_of(start * ROWS, ROWS), count * ROWS)
        total = None
        for p in range(nchol // vectors_piece):
            right = buf[slot, p * vectors_piece : (p + 1) * vectors_piece].reshape(PIECE, cols)
            product = jnp.dot(
                left[part, rows, p * PIECE : (p + 1) * PIECE], right, preferred_element_type=jnp.float32
            )
            total = product if total is None else total + product
        blocks_out[c, pl.ds(part * half + start, count)] = total.astype(jnp.bfloat16).reshape(count, ROWS, cols)

    def block_copy_at(c, r):
        return pltpu.make_async_remote_copy(
            src_ref=blocks_out.at[c, r], dst_ref=blocks_in.at[c, me], send_sem=bsend,
            recv_sem=brecv.at[c], device_id={"pb": peer_at(r)}, device_id_type=MESH,
        )

    tensor_copy(0, 0).wait()
    fetch(reach)

    def opening(fourth, carry):
        fields_of(quarter, 0, fourth).wait_recv()
        build(fourth)
        multiply(0, 0, 0, fourth * quarter, quarter)
        for r in range(quarter):
            block_copy_at(0, fourth * quarter + r).start()
        return carry

    lax.fori_loop(0, 2, opening, 0)

    paired = chunks - AHEAD

    def step(t, carry):
        later = t - AHEAD
        part = jnp.where(t < AHEAD, 0, jnp.where(later >= 2 * paired, 1, 1 - later % 2))
        c = jnp.where(t < AHEAD, t, jnp.where(later >= 2 * paired, later - paired, later // 2 + AHEAD * (later % 2)))
        slot = lax.rem(c, slots)

        @pl.when(t == AHEAD)
        def _():
            fields_of(half - 1, 1, 2).wait_recv()

            def both(fourth, carry):
                build(fourth)
                return carry

            lax.fori_loop(2, 4, both, 0)

        @pl.when(part == 0)
        def _():
            tensor_copy(c, slot).wait()

            @pl.when(c + reach < chunks)
            def _():
                tensor_copy(c + reach, lax.rem(c + reach, slots)).start()

        multiply(c, slot, part, 0, half)

        @pl.when(part == 0)
        def _():
            for r in range(quarter, half):
                block_copy(c, r).start()

            @pl.when(c > BEHIND)
            def _():
                for r in range(quarter):
                    block_copy(c - BEHIND, r).start()

        @pl.when(part == 1)
        def _():
            for r in range(half + 1, n):
                block_copy(c, r).start()
            blocks_in[c, me] = blocks_out[c, half]

            @pl.when(jnp.logical_and(c >= paired, c - paired < BEHIND))
            def _():
                for r in range(quarter):
                    block_copy(c - paired + chunks - BEHIND, r).start()

        return carry

    lax.fori_loop(1, 2 * chunks, step, 0)
    walker_copy.wait()
    others = pl.ds(0, n - 1)
    lane = lax.broadcasted_iota(jnp.int32, (ROWS, 128), 1)
    row = lax.broadcasted_iota(jnp.int32, (ROWS, 128), 0)

    def assemble(c, carry):
        h, i = c // row_blocks, c % row_blocks
        pltpu.make_async_remote_copy(
            src_ref=blocks_out.at[c, others], dst_ref=blocks_in.at[c, others], send_sem=bsend,
            recv_sem=brecv.at[c], device_id={"pb": peer_of(0)}, device_id_type=MESH,
        ).wait_recv()
        for kk in range(k_here):
            k = h * k_here + kk
            start = kk // 2 * 128
            off = kk % 2 * norb
            rows = pl.ds(pl.multiple_of(k * norb + i * ROWS, ROWS), ROWS)
            here = slice(kk * ROWS, (kk + 1) * ROWS)
            for pair in range(nk // 2):
                one = blocks_in[c, lax.rem(k - 2 * pair + nk, nk), :, start : start + 128]
                two = blocks_in[c, lax.rem(k - 2 * pair - 1 + nk, nk), :, start : start + 128]
                rows_in[here, pair * 128 : (pair + 1) * 128] = jnp.concatenate(
                    [one[:, off : off + norb], two[:, off : off + norb]], axis=1
                )
            place = pl.ds(pl.multiple_of(k // 2 * 128, 128), 128)
            extra = jnp.where(lane == row + (off + i * ROWS), jnp.broadcast_to(pairs[k // 2], (ROWS, 128)), 0.0)
            rows_in[here, place] = (rows_in[here, place].astype(jnp.float32) + extra).astype(jnp.bfloat16)
            matrix[rows, :] = rows_in[here, :]
        product = jnp.dot(rows_in[...], walker[...], preferred_element_type=jnp.float32)
        for kk in range(k_here):
            rows = pl.ds(pl.multiple_of((h * k_here + kk) * norb + i * ROWS, ROWS), ROWS)
            first[rows, :] = (-product[kk * ROWS : (kk + 1) * ROWS]).astype(jnp.bfloat16)
        return carry

    lax.fori_loop(0, chunks, assemble, 0)
    fields_of(half, 0, 0).wait_send()
    fields_of(half - 1, 1, 2).wait_send()
    pltpu.make_async_remote_copy(
        src_ref=blocks_out.at[:, others], dst_ref=blocks_in.at[:, others], send_sem=bsend,
        recv_sem=brecv.at[0], device_id={"pb": peer_of(0)}, device_id_type=MESH,
    ).wait_send()


def series(matrix, first, walker_hbm, out_hbm, walker, term_a, term_b, total, out, wsem, osem):
    size = matrix.shape[0]
    copy = pltpu.make_async_copy(walker_hbm, walker, wsem)
    copy.start()
    copies = []
    for number in range(2, TERMS):
        source = first if number == 2 else (term_a, term_b)[number % 2]
        target = (term_b, term_a)[number % 2]
        for r in range(0, size, STEP):
            rows = slice(r, r + STEP)
            product = jnp.dot(matrix[rows, :], source[...], preferred_element_type=jnp.float32)
            term = (product * (-1.0 / number)).astype(jnp.bfloat16)
            if number == 2:
                if r == 0:
                    copy.wait()
                before = walker[rows, :].astype(jnp.float32) + first[rows, :].astype(jnp.float32)
            else:
                before = total[rows, :]
            after = before + term.astype(jnp.float32)
            if number < TERMS - 1:
                target[rows, :] = term
                total[rows, :] = after
            else:
                out[rows, :] = after.astype(jnp.bfloat16)
                copies.append(pltpu.make_async_copy(out.at[rows, :], out_hbm.at[rows, :], osem.at[r // STEP]))
                copies[-1].start()
    for copy in copies:
        copy.wait()


def fused(fields, field_shift, cholesky, onebody, walkers):
    n = lax.axis_size("pb")
    nk, norb = onebody.shape
    nchol = cholesky.shape[0]
    width = cholesky.shape[2]
    cols = width // SPLITS
    chunks = norb // ROWS * SPLITS
    slots = min(SLOTS, chunks)
    size, columns = walkers.shape[1:]
    bf16, f32 = jnp.bfloat16, jnp.float32
    vmem = pl.BlockSpec(memory_space=pltpu.VMEM)
    hbm = pl.BlockSpec(memory_space=pl.ANY)
    walker = walkers.reshape(size, columns)
    matrix, first = pl.pallas_call(
        functools.partial(exchange, n, nk, norb),
        out_shape=(pltpu.VMEM((size, size), bf16), pltpu.VMEM((size, columns), bf16)),
        in_specs=[hbm] * 5,
        out_specs=(vmem, vmem),
        scratch_shapes=[
            pltpu.VMEM((nk, nchol), f32),
            pltpu.VMEM(field_shift.shape, f32),
            pltpu.VMEM((nk, norb), f32),
            pltpu.VMEM((nk, 1, nchol), f32),
            pltpu.VMEM((n, 1, nchol), f32),
            pltpu.VMEM((n // 4, nchol), f32),
            pltpu.VMEM((128, 128 * ROWS), bf16),
            pltpu.VMEM((2, n // 2 * ROWS, nchol * ROWS), bf16),
            pltpu.VMEM((slots, nchol, ROWS, cols), bf16),
            pltpu.VMEM((chunks, n, ROWS, cols), bf16),
            pltpu.VMEM((chunks, n, ROWS, cols), bf16),
            pltpu.VMEM((cols // norb * ROWS, size), bf16),
            pltpu.VMEM((nk // 2, 1, 2 * norb), f32),
            pltpu.VMEM((size, columns), bf16),
            pltpu.SemaphoreType.DMA((3,)),
            pltpu.SemaphoreType.DMA((2,)),
            pltpu.SemaphoreType.DMA((3,)),
            pltpu.SemaphoreType.DMA((slots,)),
            pltpu.SemaphoreType.DMA,
            pltpu.SemaphoreType.DMA((chunks,)),
            pltpu.SemaphoreType.DMA,
            pltpu.SemaphoreType.REGULAR((3,)),
        ],
        compiler_params=pltpu.CompilerParams(
            collective_id=0, has_side_effects=True, vmem_limit_bytes=VMEM_EXCHANGE
        ),
    )(fields.reshape(nk, nchol), field_shift, onebody, cholesky, walker)
    out = pl.pallas_call(
        series,
        out_shape=jax.ShapeDtypeStruct((size, columns), bf16),
        in_specs=[vmem, vmem, hbm],
        out_specs=hbm,
        scratch_shapes=[
            pltpu.VMEM((size, columns), bf16),
            pltpu.VMEM((size, columns), bf16),
            pltpu.VMEM((size, columns), bf16),
            pltpu.VMEM((size, columns), f32),
            pltpu.VMEM((size, columns), bf16),
            pltpu.SemaphoreType.DMA,
            pltpu.SemaphoreType.DMA((size // STEP,)),
        ],
        compiler_params=pltpu.CompilerParams(vmem_limit_bytes=VMEM_SERIES),
    )(matrix, first, walker)
    return out.reshape(walkers.shape)


def per_device(fields, field_shift, cholesky, onebody, walkers):
    n = lax.axis_size("pb")
    nk, norb = onebody.shape
    fits = (
        fields.shape[0] == 1 and n == nk and n % 4 == 0 and cholesky.shape[1] == norb and norb == 64
        and walkers.shape[2] % 128 == 0 and cholesky.shape[0] % 128 == 0
    )
    body = fused if fits else plain
    return body(fields, field_shift, cholesky, onebody, walkers)


def solution(mesh):
    return jax.shard_map(
        per_device,
        mesh=mesh,
        in_specs=(
            P(("groups", "pb"), None, None),
            P(),
            P(None, "pb", None),
            P(),
            P(("groups", "pb"), None, None),
        ),
        out_specs=P(("groups", "pb"), None, None),
        check_vma=False,
    )
```

```python
import functools

import jax
import jax.numpy as jnp
from jax import lax
from jax.experimental import pallas as pl
from jax.experimental.pallas import tpu as pltpu
from jax.sharding import PartitionSpec as P

TERMS = 6
MESH = pl.DeviceIdType.MESH
ROWS = 16
SLOTS = 8
SPLITS = 4
PIECE = 2048
STEP = 256
AHEAD = 4
FIRST = 3
BEHIND = 3
VMEM_EXCHANGE = 58 * 1024 * 1024
VMEM_SERIES = 16 * 1024 * 1024


def plain(fields, field_shift, cholesky, onebody, walkers):
    devices = lax.axis_size("pb")
    local_walkers = fields.shape[0]
    kpoints = field_shift.shape[0]
    orbitals = onebody.shape[1]
    vectors = field_shift.shape[1]
    rows_here = cholesky.shape[1]
    per_transfer = orbitals // rows_here
    slab = cholesky.reshape(vectors, rows_here * kpoints * orbitals)
    shifted = (fields + field_shift[None]).astype(jnp.bfloat16)
    outgoing = jnp.repeat(shifted, per_transfer, axis=1)
    arrived = lax.all_to_all(outgoing, "pb", split_axis=1, concat_axis=0, tiled=True)
    partial_blocks = jnp.dot(arrived[:, 0, :], slab, preferred_element_type=jnp.float32).astype(
        jnp.bfloat16
    )
    outgoing_blocks = partial_blocks.reshape(devices, local_walkers, rows_here * kpoints * orbitals)
    relayed = lax.all_to_all(outgoing_blocks, "pb", split_axis=0, concat_axis=0, tiled=True)
    relayed = relayed.reshape(kpoints, per_transfer, local_walkers, rows_here, kpoints, orbitals)
    potential = relayed.transpose(2, 4, 1, 3, 0, 5).reshape(
        local_walkers, kpoints, orbitals, kpoints, orbitals
    )
    turned = jnp.flip(potential, axis=3)
    permuted = jnp.stack(
        [jnp.roll(turned[:, k], k + 1, axis=2) for k in range(kpoints)], axis=1
    )
    permuted = permuted.reshape(local_walkers, kpoints * orbitals, kpoints * orbitals)
    diagonal_term = onebody.reshape(kpoints * orbitals)[None, :, None]
    term = walkers
    total = term.astype(jnp.float32)
    for order in range(1, TERMS):
        product = jnp.einsum("wij,wjc->wic", permuted, term, preferred_element_type=jnp.float32)
        product = product + diagonal_term * term.astype(jnp.float32)
        term = (product * (-1.0 / order)).astype(jnp.bfloat16)
        total = total + term.astype(jnp.float32)
    return total.astype(jnp.bfloat16)


def exchange(
    n, nk, norb, fields_hbm, shift_hbm, onebody_hbm, chol_hbm, walker_hbm, matrix, first, partial,
    fields, shift, onebody, fields_out, fields_in, lines, spread, left, buf, blocks_out, blocks_in, rows_in,
    pairs, walker, fsem, fsend, frecv, csem, bsend, brecv, wsem, ready,
):
    me = lax.axis_index("pb")
    nchol = chol_hbm.shape[0]
    width = chol_hbm.shape[2]
    cols = buf.shape[3]
    slots = buf.shape[0]
    row_blocks = norb // ROWS
    chunks = row_blocks * (width // cols)
    reach = slots - AHEAD
    k_here = cols // norb
    group = 128
    wide = group * ROWS
    half, quarter = n // 2, n // 4
    mine = me // half
    places = [r for r in range(n) if r != half]

    def peer_of(r):
        if r < half:
            row = 2 - mine if r < quarter else 3 * (1 - mine)
            return row * quarter + lax.rem(me + r, quarter)
        return mine * half + lax.rem(me + r, half)

    def tensor_copy(c, slot):
        h, i = c // row_blocks, c % row_blocks
        return pltpu.make_async_copy(
            chol_hbm.at[:, pl.ds(pl.multiple_of(i * ROWS, ROWS), ROWS), pl.ds(pl.multiple_of(h * cols, cols), cols)],
            buf.at[slot],
            csem.at[slot],
        )

    def peer_at(r):
        far = jnp.where(r < quarter, 2 - mine, 3 * (1 - mine)) * quarter + lax.rem(me + r, quarter)
        return jnp.where(r < half, far, mine * half + lax.rem(me + r, half))

    def fetch(c):
        if c < chunks:
            tensor_copy(c, c % slots).start()

    barrier = pltpu.get_barrier_semaphore()
    for r in places:
        peer = peer_of(r)

        @pl.when(peer > me)
        def _():
            pl.semaphore_signal(barrier, inc=1, device_id={"pb": peer}, device_id_type=MESH)

    small = [
        pltpu.make_async_copy(fields_hbm, fields, fsem.at[0]),
        pltpu.make_async_copy(shift_hbm, shift, fsem.at[1]),
        pltpu.make_async_copy(onebody_hbm, onebody, fsem.at[2]),
    ]
    for copy in small:
        copy.start()
    for c in range(FIRST):
        fetch(c)
    walker_copy = pltpu.make_async_copy(walker_hbm, walker, wsem)
    walker_copy.start()
    small[0].wait()
    for q in range(nk):
        fields_out[q] = fields[q : q + 1, :]
    fields_in[me] = fields_out[me]
    spread[...] = (
        lax.broadcasted_iota(jnp.int32, (group, wide), 1) // ROWS
        == lax.broadcasted_iota(jnp.int32, (group, wide), 0)
    ).astype(jnp.float32).astype(jnp.bfloat16)
    for copy in small[1:]:
        copy.wait()
    for k in range(nk):
        pairs[k // 2, :, k % 2 * norb : (k % 2 + 1) * norb] = onebody[k : k + 1, :]

    kind = jnp.where((me // quarter) % 3 == 0, 1, 0)

    def field_copy(r):
        peer = peer_of(r)
        return pltpu.make_async_remote_copy(
            src_ref=fields_out.at[peer], dst_ref=fields_in.at[me], send_sem=fsend.at[0 if r < half else 1],
            recv_sem=frecv.at[kind if r < half else 2], device_id={"pb": peer}, device_id_type=MESH,
        )

    def fields_of(count, send, number):
        some = pl.ds(0, count)
        return pltpu.make_async_remote_copy(
            src_ref=fields_out.at[some], dst_ref=fields_in.at[some], send_sem=fsend.at[send],
            recv_sem=frecv.at[number], device_id={"pb": peer_of(0)}, device_id_type=MESH,
        )


    @pl.when(me > 0)
    def _():
        pl.semaphore_wait(barrier, me)

    late = (me // quarter) % 2

    @pl.when(mine == 1)
    def _():
        for r in [*range(quarter), *range(quarter, half)]:
            pl.semaphore_signal(ready.at[late], inc=1, device_id={"pb": peer_of(r)}, device_id_type=MESH)
        for r in range(half):
            field_copy(r).start()

    for r in range(half + 1, n):
        peer = peer_of(r)

        @pl.when(peer < me)
        def _():
            pl.semaphore_signal(ready.at[2], inc=1, device_id={"pb": peer}, device_id_type=MESH)

    @pl.when(mine == 0)
    def _():
        for part in range(2):
            pl.semaphore_wait(ready.at[part], quarter)
            for r in range(part * quarter, (part + 1) * quarter):
                field_copy(r).start()

    above = half - 1 - lax.rem(me, half)

    @pl.when(above > 0)
    def _():
        pl.semaphore_wait(ready.at[2], above)

    for r in range(half + 1, n):
        field_copy(r).start()
    for c in range(FIRST, reach):
        fetch(c)

    mask = (
        lax.broadcasted_iota(jnp.int32, (ROWS, wide), 1) % ROWS
        == lax.broadcasted_iota(jnp.int32, (ROWS, wide), 0)
    )

    def block_copy(c, r):
        peer = peer_of(r)
        return pltpu.make_async_remote_copy(
            src_ref=blocks_out.at[c, r], dst_ref=blocks_in.at[c, me], send_sem=bsend,
            recv_sem=brecv.at[c], device_id={"pb": peer}, device_id_type=MESH,
        )

    vectors_piece = PIECE // ROWS

    def build(fourth):
        for r in range(quarter):
            lines[r : r + 1, :] = fields_in[peer_at(fourth * quarter + r)]
        shifted = (lines[...] + shift[pl.ds(me, 1), :]).astype(jnp.bfloat16)
        for b in range(nchol // group):
            spreaded = jnp.dot(
                shifted[:, b * group : (b + 1) * group], spread[...],
                preferred_element_type=jnp.float32,
            )
            for r in range(quarter):
                line = jnp.broadcast_to(spreaded[r : r + 1, :], (ROWS, wide))
                start = (fourth % 2 * quarter + r) * ROWS
                left[fourth // 2, pl.ds(pl.multiple_of(start, ROWS), ROWS), b * wide : (b + 1) * wide] = jnp.where(
                    mask, line, 0.0
                ).astype(jnp.bfloat16)

    def multiply(c, slot, part, start, count):
        rows = pl.ds(pl.multiple_of(start * ROWS, ROWS), count * ROWS)
        total = None
        for p in range(nchol // vectors_piece):
            right = buf[slot, p * vectors_piece : (p + 1) * vectors_piece].reshape(PIECE, cols)
            product = jnp.dot(
                left[part, rows, p * PIECE : (p + 1) * PIECE], right, preferred_element_type=jnp.float32
            )
            total = product if total is None else total + product
        blocks_out[c, pl.ds(part * half + start, count)] = total.astype(jnp.bfloat16).reshape(count, ROWS, cols)

    def block_copy_at(c, r):
        return pltpu.make_async_remote_copy(
            src_ref=blocks_out.at[c, r], dst_ref=blocks_in.at[c, me], send_sem=bsend,
            recv_sem=brecv.at[c], device_id={"pb": peer_at(r)}, device_id_type=MESH,
        )

    tensor_copy(0, 0).wait()
    fetch(reach)

    def opening(fourth, carry):
        fields_of(quarter, 0, fourth).wait_recv()
        build(fourth)
        multiply(0, 0, 0, fourth * quarter, quarter)
        for r in range(quarter):
            block_copy_at(0, fourth * quarter + r).start()
        return carry

    lax.fori_loop(0, 2, opening, 0)

    paired = chunks - AHEAD

    def step(t, carry):
        later = t - AHEAD
        part = jnp.where(t < AHEAD, 0, jnp.where(later >= 2 * paired, 1, 1 - later % 2))
        c = jnp.where(t < AHEAD, t, jnp.where(later >= 2 * paired, later - paired, later // 2 + AHEAD * (later % 2)))
        slot = lax.rem(c, slots)

        @pl.when(t == AHEAD)
        def _():
            fields_of(half - 1, 1, 2).wait_recv()

            def both(fourth, carry):
                build(fourth)
                return carry

            lax.fori_loop(2, 4, both, 0)

        @pl.when(part == 0)
        def _():
            tensor_copy(c, slot).wait()

            @pl.when(c + reach < chunks)
            def _():
                tensor_copy(c + reach, lax.rem(c + reach, slots)).start()

        multiply(c, slot, part, 0, half)

        @pl.when(part == 0)
        def _():
            for r in range(quarter, half):
                block_copy(c, r).start()

            @pl.when(c > BEHIND)
            def _():
                for r in range(quarter):
                    block_copy(c - BEHIND, r).start()

        @pl.when(part == 1)
        def _():
            for r in range(half + 1, n):
                block_copy(c, r).start()
            blocks_in[c, me] = blocks_out[c, half]

            @pl.when(jnp.logical_and(c >= paired, c - paired < BEHIND))
            def _():
                for r in range(quarter):
                    block_copy(c - paired + chunks - BEHIND, r).start()

        return carry

    lax.fori_loop(1, 2 * chunks, step, 0)
    walker_copy.wait()
    others = pl.ds(0, n - 1)
    lane = lax.broadcasted_iota(jnp.int32, (ROWS, 128), 1)
    row = lax.broadcasted_iota(jnp.int32, (ROWS, 128), 0)

    def assemble(c, carry):
        h, i = c // row_blocks, c % row_blocks
        pltpu.make_async_remote_copy(
            src_ref=blocks_out.at[c, others], dst_ref=blocks_in.at[c, others], send_sem=bsend,
            recv_sem=brecv.at[c], device_id={"pb": peer_of(0)}, device_id_type=MESH,
        ).wait_recv()
        for kk in range(k_here):
            k = h * k_here + kk
            start = kk // 2 * 128
            off = kk % 2 * norb
            rows = pl.ds(pl.multiple_of(k * norb + i * ROWS, ROWS), ROWS)
            here = slice(kk * ROWS, (kk + 1) * ROWS)
            for pair in range(nk // 2):
                one = blocks_in[c, lax.rem(k - 2 * pair + nk, nk), :, start : start + 128]
                two = blocks_in[c, lax.rem(k - 2 * pair - 1 + nk, nk), :, start : start + 128]
                rows_in[here, pair * 128 : (pair + 1) * 128] = jnp.concatenate(
                    [one[:, off : off + norb], two[:, off : off + norb]], axis=1
                )
            place = pl.ds(pl.multiple_of(k // 2 * 128, 128), 128)
            extra = jnp.where(lane == row + (off + i * ROWS), jnp.broadcast_to(pairs[k // 2], (ROWS, 128)), 0.0)
            rows_in[here, place] = (rows_in[here, place].astype(jnp.float32) + extra).astype(jnp.bfloat16)
            matrix[rows, :] = rows_in[here, :]
        product = jnp.dot(rows_in[...], walker[...], preferred_element_type=jnp.float32)
        for kk in range(k_here):
            rows = pl.ds(pl.multiple_of((h * k_here + kk) * norb + i * ROWS, ROWS), ROWS)
            first[rows, :] = (-product[kk * ROWS : (kk + 1) * ROWS]).astype(jnp.bfloat16)

        @pl.when(c == width // cols * row_blocks - row_blocks - 1)
        def _():
            known = partial.shape[0]
            for r in range(0, known, STEP):
                partial[r : r + STEP, :] = jnp.dot(
                    matrix[r : r + STEP, :known], first[:known, :], preferred_element_type=jnp.float32
                )

        return carry

    lax.fori_loop(0, chunks, assemble, 0)
    fields_of(half, 0, 0).wait_send()
    fields_of(half - 1, 1, 2).wait_send()
    pltpu.make_async_remote_copy(
        src_ref=blocks_out.at[:, others], dst_ref=blocks_in.at[:, others], send_sem=bsend,
        recv_sem=brecv.at[0], device_id={"pb": peer_of(0)}, device_id_type=MESH,
    ).wait_send()


def series(matrix, first, partial, walker_hbm, out_hbm, walker, term_a, term_b, total, out, wsem, osem):
    size = matrix.shape[0]
    copy = pltpu.make_async_copy(walker_hbm, walker, wsem)
    copy.start()
    copies = []
    for number in range(2, TERMS):
        source = first if number == 2 else (term_a, term_b)[number % 2]
        target = (term_b, term_a)[number % 2]
        for r in range(0, size, STEP):
            rows = slice(r, r + STEP)
            known = partial.shape[0] if number == 2 and r < partial.shape[0] else 0
            product = jnp.dot(matrix[rows, known:], source[known:, :], preferred_element_type=jnp.float32)
            if known:
                product += partial[rows, :]
            term = (product * (-1.0 / number)).astype(jnp.bfloat16)
            if number == 2:
                if r == 0:
                    copy.wait()
                before = walker[rows, :].astype(jnp.float32) + first[rows, :].astype(jnp.float32)
            else:
                before = total[rows, :]
            after = before + term.astype(jnp.float32)
            if number < TERMS - 1:
                target[rows, :] = term
                total[rows, :] = after
            else:
                out[rows, :] = after.astype(jnp.bfloat16)
                copies.append(pltpu.make_async_copy(out.at[rows, :], out_hbm.at[rows, :], osem.at[r // STEP]))
                copies[-1].start()
    for copy in copies:
        copy.wait()


def fused(fields, field_shift, cholesky, onebody, walkers):
    n = lax.axis_size("pb")
    nk, norb = onebody.shape
    nchol = cholesky.shape[0]
    width = cholesky.shape[2]
    cols = width // SPLITS
    chunks = norb // ROWS * SPLITS
    slots = min(SLOTS, chunks)
    size, columns = walkers.shape[1:]
    bf16, f32 = jnp.bfloat16, jnp.float32
    vmem = pl.BlockSpec(memory_space=pltpu.VMEM)
    hbm = pl.BlockSpec(memory_space=pl.ANY)
    walker = walkers.reshape(size, columns)
    matrix, first, partial = pl.pallas_call(
        functools.partial(exchange, n, nk, norb),
        out_shape=(
            pltpu.VMEM((size, size), bf16), pltpu.VMEM((size, columns), bf16), pltpu.VMEM((size - cols, columns), f32)
        ),
        in_specs=[hbm] * 5,
        out_specs=(vmem, vmem, vmem),
        scratch_shapes=[
            pltpu.VMEM((nk, nchol), f32),
            pltpu.VMEM(field_shift.shape, f32),
            pltpu.VMEM((nk, norb), f32),
            pltpu.VMEM((nk, 1, nchol), f32),
            pltpu.VMEM((n, 1, nchol), f32),
            pltpu.VMEM((n // 4, nchol), f32),
            pltpu.VMEM((128, 128 * ROWS), bf16),
            pltpu.VMEM((2, n // 2 * ROWS, nchol * ROWS), bf16),
            pltpu.VMEM((slots, nchol, ROWS, cols), bf16),
            pltpu.VMEM((chunks, n, ROWS, cols), bf16),
            pltpu.VMEM((chunks, n, ROWS, cols), bf16),
            pltpu.VMEM((cols // norb * ROWS, size), bf16),
            pltpu.VMEM((nk // 2, 1, 2 * norb), f32),
            pltpu.VMEM((size, columns), bf16),
            pltpu.SemaphoreType.DMA((3,)),
            pltpu.SemaphoreType.DMA((2,)),
            pltpu.SemaphoreType.DMA((3,)),
            pltpu.SemaphoreType.DMA((slots,)),
            pltpu.SemaphoreType.DMA,
            pltpu.SemaphoreType.DMA((chunks,)),
            pltpu.SemaphoreType.DMA,
            pltpu.SemaphoreType.REGULAR((3,)),
        ],
        compiler_params=pltpu.CompilerParams(
            collective_id=0, has_side_effects=True, vmem_limit_bytes=VMEM_EXCHANGE
        ),
    )(fields.reshape(nk, nchol), field_shift, onebody, cholesky, walker)
    out = pl.pallas_call(
        series,
        out_shape=jax.ShapeDtypeStruct((size, columns), bf16),
        in_specs=[vmem, vmem, vmem, hbm],
        out_specs=hbm,
        scratch_shapes=[
            pltpu.VMEM((size, columns), bf16),
            pltpu.VMEM((size, columns), bf16),
            pltpu.VMEM((size, columns), bf16),
            pltpu.VMEM((size, columns), f32),
            pltpu.VMEM((size, columns), bf16),
            pltpu.SemaphoreType.DMA,
            pltpu.SemaphoreType.DMA((size // STEP,)),
        ],
        compiler_params=pltpu.CompilerParams(vmem_limit_bytes=VMEM_SERIES),
    )(matrix, first, partial, walker)
    return out.reshape(walkers.shape)


def per_device(fields, field_shift, cholesky, onebody, walkers):
    n = lax.axis_size("pb")
    nk, norb = onebody.shape
    fits = (
        fields.shape[0] == 1 and n == nk and n % 4 == 0 and cholesky.shape[1] == norb and norb == 64
        and walkers.shape[2] % 128 == 0 and cholesky.shape[0] % 128 == 0
        and cholesky.shape[2] % (SPLITS * STEP) == 0
    )
    body = fused if fits else plain
    return body(fields, field_shift, cholesky, onebody, walkers)


def solution(mesh):
    return jax.shard_map(
        per_device,
        mesh=mesh,
        in_specs=(
            P(("groups", "pb"), None, None),
            P(),
            P(None, "pb", None),
            P(),
            P(("groups", "pb"), None, None),
        ),
        out_specs=P(("groups", "pb"), None, None),
        check_vma=False,
    )
```

```python
import functools

import jax
import jax.numpy as jnp
from jax import lax
from jax.experimental import pallas as pl
from jax.experimental.pallas import tpu as pltpu
from jax.sharding import PartitionSpec as P

TERMS = 6
MESH = pl.DeviceIdType.MESH
ROWS = 16
SLOTS = 8
SPLITS = 4
PIECE = 2048
STEP = 256
AHEAD = 5
FIRST = 3
BEHIND = 3
VMEM_EXCHANGE = 58 * 1024 * 1024
VMEM_SERIES = 16 * 1024 * 1024


def plain(fields, field_shift, cholesky, onebody, walkers):
    devices = lax.axis_size("pb")
    local_walkers = fields.shape[0]
    kpoints = field_shift.shape[0]
    orbitals = onebody.shape[1]
    vectors = field_shift.shape[1]
    rows_here = cholesky.shape[1]
    per_transfer = orbitals // rows_here
    slab = cholesky.reshape(vectors, rows_here * kpoints * orbitals)
    shifted = (fields + field_shift[None]).astype(jnp.bfloat16)
    outgoing = jnp.repeat(shifted, per_transfer, axis=1)
    arrived = lax.all_to_all(outgoing, "pb", split_axis=1, concat_axis=0, tiled=True)
    partial_blocks = jnp.dot(arrived[:, 0, :], slab, preferred_element_type=jnp.float32).astype(
        jnp.bfloat16
    )
    outgoing_blocks = partial_blocks.reshape(devices, local_walkers, rows_here * kpoints * orbitals)
    relayed = lax.all_to_all(outgoing_blocks, "pb", split_axis=0, concat_axis=0, tiled=True)
    relayed = relayed.reshape(kpoints, per_transfer, local_walkers, rows_here, kpoints, orbitals)
    potential = relayed.transpose(2, 4, 1, 3, 0, 5).reshape(
        local_walkers, kpoints, orbitals, kpoints, orbitals
    )
    turned = jnp.flip(potential, axis=3)
    permuted = jnp.stack(
        [jnp.roll(turned[:, k], k + 1, axis=2) for k in range(kpoints)], axis=1
    )
    permuted = permuted.reshape(local_walkers, kpoints * orbitals, kpoints * orbitals)
    diagonal_term = onebody.reshape(kpoints * orbitals)[None, :, None]
    term = walkers
    total = term.astype(jnp.float32)
    for order in range(1, TERMS):
        product = jnp.einsum("wij,wjc->wic", permuted, term, preferred_element_type=jnp.float32)
        product = product + diagonal_term * term.astype(jnp.float32)
        term = (product * (-1.0 / order)).astype(jnp.bfloat16)
        total = total + term.astype(jnp.float32)
    return total.astype(jnp.bfloat16)


def exchange(
    n, nk, norb, fields_hbm, shift_hbm, onebody_hbm, chol_hbm, walker_hbm, matrix, first, partial,
    fields, shift, onebody, fields_out, fields_in, lines, spread, left, buf, blocks_out, blocks_in, rows_in,
    pairs, walker, fsem, fsend, frecv, csem, bsend, brecv, wsem, ready,
):
    me = lax.axis_index("pb")
    nchol = chol_hbm.shape[0]
    width = chol_hbm.shape[2]
    cols = buf.shape[3]
    slots = buf.shape[0]
    row_blocks = norb // ROWS
    chunks = row_blocks * (width // cols)
    reach = slots - AHEAD
    k_here = cols // norb
    group = 128
    wide = group * ROWS
    half, quarter = n // 2, n // 4
    mine = me // half
    places = [r for r in range(n) if r != half]

    def peer_of(r):
        if r < half:
            row = 2 - mine if r < quarter else 3 * (1 - mine)
            return row * quarter + lax.rem(me + r, quarter)
        return mine * half + lax.rem(me + r, half)

    def tensor_copy(c, slot):
        h, i = c // row_blocks, c % row_blocks
        return pltpu.make_async_copy(
            chol_hbm.at[:, pl.ds(pl.multiple_of(i * ROWS, ROWS), ROWS), pl.ds(pl.multiple_of(h * cols, cols), cols)],
            buf.at[slot],
            csem.at[slot],
        )

    def peer_at(r):
        far = jnp.where(r < quarter, 2 - mine, 3 * (1 - mine)) * quarter + lax.rem(me + r, quarter)
        return jnp.where(r < half, far, mine * half + lax.rem(me + r, half))

    def fetch(c):
        if c < chunks:
            tensor_copy(c, c % slots).start()

    barrier = pltpu.get_barrier_semaphore()
    for r in places:
        peer = peer_of(r)

        @pl.when(peer > me)
        def _():
            pl.semaphore_signal(barrier, inc=1, device_id={"pb": peer}, device_id_type=MESH)

    small = [
        pltpu.make_async_copy(fields_hbm, fields, fsem.at[0]),
        pltpu.make_async_copy(shift_hbm, shift, fsem.at[1]),
        pltpu.make_async_copy(onebody_hbm, onebody, fsem.at[2]),
    ]
    for copy in small:
        copy.start()
    for c in range(FIRST):
        fetch(c)
    walker_copy = pltpu.make_async_copy(walker_hbm, walker, wsem)
    walker_copy.start()
    small[0].wait()
    for q in range(nk):
        fields_out[q] = fields[q : q + 1, :]
    fields_in[me] = fields_out[me]
    spread[...] = (
        lax.broadcasted_iota(jnp.int32, (group, wide), 1) // ROWS
        == lax.broadcasted_iota(jnp.int32, (group, wide), 0)
    ).astype(jnp.float32).astype(jnp.bfloat16)
    for copy in small[1:]:
        copy.wait()
    for k in range(nk):
        pairs[k // 2, :, k % 2 * norb : (k % 2 + 1) * norb] = onebody[k : k + 1, :]

    kind = jnp.where((me // quarter) % 3 == 0, 1, 0)

    def field_copy(r):
        peer = peer_of(r)
        return pltpu.make_async_remote_copy(
            src_ref=fields_out.at[peer], dst_ref=fields_in.at[me], send_sem=fsend.at[0 if r < half else 1],
            recv_sem=frecv.at[kind if r < half else 2], device_id={"pb": peer}, device_id_type=MESH,
        )

    def fields_of(count, send, number):
        some = pl.ds(0, count)
        return pltpu.make_async_remote_copy(
            src_ref=fields_out.at[some], dst_ref=fields_in.at[some], send_sem=fsend.at[send],
            recv_sem=frecv.at[number], device_id={"pb": peer_of(0)}, device_id_type=MESH,
        )


    @pl.when(me > 0)
    def _():
        pl.semaphore_wait(barrier, me)

    late = (me // quarter) % 2

    @pl.when(mine == 1)
    def _():
        for r in [*range(quarter), *range(quarter, half)]:
            pl.semaphore_signal(ready.at[late], inc=1, device_id={"pb": peer_of(r)}, device_id_type=MESH)
        for r in range(half):
            field_copy(r).start()

    for r in range(half + 1, n):
        peer = peer_of(r)

        @pl.when(peer < me)
        def _():
            pl.semaphore_signal(ready.at[2], inc=1, device_id={"pb": peer}, device_id_type=MESH)

    @pl.when(mine == 0)
    def _():
        for part in range(2):
            pl.semaphore_wait(ready.at[part], quarter)
            for r in range(part * quarter, (part + 1) * quarter):
                field_copy(r).start()

    above = half - 1 - lax.rem(me, half)

    @pl.when(above > 0)
    def _():
        pl.semaphore_wait(ready.at[2], above)

    for r in range(half + 1, n):
        field_copy(r).start()
    for c in range(FIRST, reach):
        fetch(c)

    mask = (
        lax.broadcasted_iota(jnp.int32, (ROWS, wide), 1) % ROWS
        == lax.broadcasted_iota(jnp.int32, (ROWS, wide), 0)
    )

    def block_copy(c, r):
        peer = peer_of(r)
        return pltpu.make_async_remote_copy(
            src_ref=blocks_out.at[c, r], dst_ref=blocks_in.at[c, me], send_sem=bsend,
            recv_sem=brecv.at[c], device_id={"pb": peer}, device_id_type=MESH,
        )

    vectors_piece = PIECE // ROWS

    def build(fourth):
        for r in range(quarter):
            lines[r : r + 1, :] = fields_in[peer_at(fourth * quarter + r)]
        shifted = (lines[...] + shift[pl.ds(me, 1), :]).astype(jnp.bfloat16)
        for b in range(nchol // group):
            spreaded = jnp.dot(
                shifted[:, b * group : (b + 1) * group], spread[...],
                preferred_element_type=jnp.float32,
            )
            for r in range(quarter):
                line = jnp.broadcast_to(spreaded[r : r + 1, :], (ROWS, wide))
                start = (fourth % 2 * quarter + r) * ROWS
                left[fourth // 2, pl.ds(pl.multiple_of(start, ROWS), ROWS), b * wide : (b + 1) * wide] = jnp.where(
                    mask, line, 0.0
                ).astype(jnp.bfloat16)

    def multiply(c, slot, part, start, count):
        rows = pl.ds(pl.multiple_of(start * ROWS, ROWS), count * ROWS)
        total = None
        for p in range(nchol // vectors_piece):
            right = buf[slot, p * vectors_piece : (p + 1) * vectors_piece].reshape(PIECE, cols)
            product = jnp.dot(
                left[part, rows, p * PIECE : (p + 1) * PIECE], right, preferred_element_type=jnp.float32
            )
            total = product if total is None else total + product
        blocks_out[c, pl.ds(part * half + start, count)] = total.astype(jnp.bfloat16).reshape(count, ROWS, cols)

    def block_copy_at(c, r):
        return pltpu.make_async_remote_copy(
            src_ref=blocks_out.at[c, r], dst_ref=blocks_in.at[c, me], send_sem=bsend,
            recv_sem=brecv.at[c], device_id={"pb": peer_at(r)}, device_id_type=MESH,
        )

    tensor_copy(0, 0).wait()
    fetch(reach)

    def opening(fourth, carry):
        fields_of(quarter, 0, fourth).wait_recv()
        build(fourth)
        multiply(0, 0, 0, fourth * quarter, quarter)
        for r in range(quarter):
            block_copy_at(0, fourth * quarter + r).start()
        return carry

    lax.fori_loop(0, 2, opening, 0)

    paired = chunks - AHEAD

    def step(t, carry):
        later = t - AHEAD
        part = jnp.where(t < AHEAD, 0, jnp.where(later >= 2 * paired, 1, 1 - later % 2))
        c = jnp.where(t < AHEAD, t, jnp.where(later >= 2 * paired, later - paired, later // 2 + AHEAD * (later % 2)))
        slot = lax.rem(c, slots)

        @pl.when(t == AHEAD)
        def _():
            fields_of(half - 1, 1, 2).wait_recv()

            def both(fourth, carry):
                build(fourth)
                return carry

            lax.fori_loop(2, 4, both, 0)

        @pl.when(part == 0)
        def _():
            tensor_copy(c, slot).wait()

            @pl.when(c + reach < chunks)
            def _():
                tensor_copy(c + reach, lax.rem(c + reach, slots)).start()

        multiply(c, slot, part, 0, half)

        @pl.when(part == 0)
        def _():
            for r in range(quarter, half):
                block_copy(c, r).start()

            @pl.when(c > BEHIND)
            def _():
                for r in range(quarter):
                    block_copy(c - BEHIND, r).start()

        @pl.when(part == 1)
        def _():
            for r in range(half + 1, n):
                block_copy(c, r).start()
            blocks_in[c, me] = blocks_out[c, half]

            @pl.when(jnp.logical_and(c >= paired, c - paired < BEHIND))
            def _():
                for r in range(quarter):
                    block_copy(c - paired + chunks - BEHIND, r).start()

        return carry

    lax.fori_loop(1, 2 * chunks, step, 0)
    walker_copy.wait()
    others = pl.ds(0, n - 1)
    lane = lax.broadcasted_iota(jnp.int32, (ROWS, 128), 1)
    row = lax.broadcasted_iota(jnp.int32, (ROWS, 128), 0)

    def assemble(c, carry):
        h, i = c // row_blocks, c % row_blocks
        pltpu.make_async_remote_copy(
            src_ref=blocks_out.at[c, others], dst_ref=blocks_in.at[c, others], send_sem=bsend,
            recv_sem=brecv.at[c], device_id={"pb": peer_of(0)}, device_id_type=MESH,
        ).wait_recv()
        for kk in range(k_here):
            k = h * k_here + kk
            start = kk // 2 * 128
            off = kk % 2 * norb
            rows = pl.ds(pl.multiple_of(k * norb + i * ROWS, ROWS), ROWS)
            here = slice(kk * ROWS, (kk + 1) * ROWS)
            for pair in range(nk // 2):
                one = blocks_in[c, lax.rem(k - 2 * pair + nk, nk), :, start : start + 128]
                two = blocks_in[c, lax.rem(k - 2 * pair - 1 + nk, nk), :, start : start + 128]
                rows_in[here, pair * 128 : (pair + 1) * 128] = jnp.concatenate(
                    [one[:, off : off + norb], two[:, off : off + norb]], axis=1
                )
            place = pl.ds(pl.multiple_of(k // 2 * 128, 128), 128)
            extra = jnp.where(lane == row + (off + i * ROWS), jnp.broadcast_to(pairs[k // 2], (ROWS, 128)), 0.0)
            rows_in[here, place] = (rows_in[here, place].astype(jnp.float32) + extra).astype(jnp.bfloat16)
            matrix[rows, :] = rows_in[here, :]
        product = jnp.dot(rows_in[...], walker[...], preferred_element_type=jnp.float32)
        for kk in range(k_here):
            rows = pl.ds(pl.multiple_of((h * k_here + kk) * norb + i * ROWS, ROWS), ROWS)
            first[rows, :] = (-product[kk * ROWS : (kk + 1) * ROWS]).astype(jnp.bfloat16)

        @pl.when(c == width // cols * row_blocks - row_blocks - 1)
        def _():
            known = partial.shape[0]
            for r in range(0, known, STEP):
                partial[r : r + STEP, :] = jnp.dot(
                    matrix[r : r + STEP, :known], first[:known, :], preferred_element_type=jnp.float32
                )

        return carry

    lax.fori_loop(0, chunks, assemble, 0)
    fields_of(half, 0, 0).wait_send()
    fields_of(half - 1, 1, 2).wait_send()
    pltpu.make_async_remote_copy(
        src_ref=blocks_out.at[:, others], dst_ref=blocks_in.at[:, others], send_sem=bsend,
        recv_sem=brecv.at[0], device_id={"pb": peer_of(0)}, device_id_type=MESH,
    ).wait_send()


def series(matrix, first, partial, walker_hbm, out_hbm, walker, term_a, term_b, total, out, wsem, osem):
    size = matrix.shape[0]
    copy = pltpu.make_async_copy(walker_hbm, walker, wsem)
    copy.start()
    copies = []
    for number in range(2, TERMS):
        source = first if number == 2 else (term_a, term_b)[number % 2]
        target = (term_b, term_a)[number % 2]
        for r in range(0, size, STEP):
            rows = slice(r, r + STEP)
            known = partial.shape[0] if number == 2 and r < partial.shape[0] else 0
            product = jnp.dot(matrix[rows, known:], source[known:, :], preferred_element_type=jnp.float32)
            if known:
                product += partial[rows, :]
            term = (product * (-1.0 / number)).astype(jnp.bfloat16)
            if number == 2:
                if r == 0:
                    copy.wait()
                before = walker[rows, :].astype(jnp.float32) + first[rows, :].astype(jnp.float32)
            else:
                before = total[rows, :]
            after = before + term.astype(jnp.float32)
            if number < TERMS - 1:
                target[rows, :] = term
                total[rows, :] = after
            else:
                out[rows, :] = after.astype(jnp.bfloat16)
                copies.append(pltpu.make_async_copy(out.at[rows, :], out_hbm.at[rows, :], osem.at[r // STEP]))
                copies[-1].start()
    for copy in copies:
        copy.wait()


def fused(fields, field_shift, cholesky, onebody, walkers):
    n = lax.axis_size("pb")
    nk, norb = onebody.shape
    nchol = cholesky.shape[0]
    width = cholesky.shape[2]
    cols = width // SPLITS
    chunks = norb // ROWS * SPLITS
    slots = min(SLOTS, chunks)
    size, columns = walkers.shape[1:]
    bf16, f32 = jnp.bfloat16, jnp.float32
    vmem = pl.BlockSpec(memory_space=pltpu.VMEM)
    hbm = pl.BlockSpec(memory_space=pl.ANY)
    walker = walkers.reshape(size, columns)
    matrix, first, partial = pl.pallas_call(
        functools.partial(exchange, n, nk, norb),
        out_shape=(
            pltpu.VMEM((size, size), bf16), pltpu.VMEM((size, columns), bf16), pltpu.VMEM((size - cols, columns), f32)
        ),
        in_specs=[hbm] * 5,
        out_specs=(vmem, vmem, vmem),
        scratch_shapes=[
            pltpu.VMEM((nk, nchol), f32),
            pltpu.VMEM(field_shift.shape, f32),
            pltpu.VMEM((nk, norb), f32),
            pltpu.VMEM((nk, 1, nchol), f32),
            pltpu.VMEM((n, 1, nchol), f32),
            pltpu.VMEM((n // 4, nchol), f32),
            pltpu.VMEM((128, 128 * ROWS), bf16),
            pltpu.VMEM((2, n // 2 * ROWS, nchol * ROWS), bf16),
            pltpu.VMEM((slots, nchol, ROWS, cols), bf16),
            pltpu.VMEM((chunks, n, ROWS, cols), bf16),
            pltpu.VMEM((chunks, n, ROWS, cols), bf16),
            pltpu.VMEM((cols // norb * ROWS, size), bf16),
            pltpu.VMEM((nk // 2, 1, 2 * norb), f32),
            pltpu.VMEM((size, columns), bf16),
            pltpu.SemaphoreType.DMA((3,)),
            pltpu.SemaphoreType.DMA((2,)),
            pltpu.SemaphoreType.DMA((3,)),
            pltpu.SemaphoreType.DMA((slots,)),
            pltpu.SemaphoreType.DMA,
            pltpu.SemaphoreType.DMA((chunks,)),
            pltpu.SemaphoreType.DMA,
            pltpu.SemaphoreType.REGULAR((3,)),
        ],
        compiler_params=pltpu.CompilerParams(
            collective_id=0, has_side_effects=True, vmem_limit_bytes=VMEM_EXCHANGE
        ),
    )(fields.reshape(nk, nchol), field_shift, onebody, cholesky, walker)
    out = pl.pallas_call(
        series,
        out_shape=jax.ShapeDtypeStruct((size, columns), bf16),
        in_specs=[vmem, vmem, vmem, hbm],
        out_specs=hbm,
        scratch_shapes=[
            pltpu.VMEM((size, columns), bf16),
            pltpu.VMEM((size, columns), bf16),
            pltpu.VMEM((size, columns), bf16),
            pltpu.VMEM((size, columns), f32),
            pltpu.VMEM((size, columns), bf16),
            pltpu.SemaphoreType.DMA,
            pltpu.SemaphoreType.DMA((size // STEP,)),
        ],
        compiler_params=pltpu.CompilerParams(vmem_limit_bytes=VMEM_SERIES),
    )(matrix, first, partial, walker)
    return out.reshape(walkers.shape)


def per_device(fields, field_shift, cholesky, onebody, walkers):
    n = lax.axis_size("pb")
    nk, norb = onebody.shape
    fits = (
        fields.shape[0] == 1 and n == nk and n % 4 == 0 and cholesky.shape[1] == norb and norb == 64
        and walkers.shape[2] % 128 == 0 and cholesky.shape[0] % 128 == 0
        and cholesky.shape[2] % (SPLITS * STEP) == 0
    )
    body = fused if fits else plain
    return body(fields, field_shift, cholesky, onebody, walkers)


def solution(mesh):
    return jax.shard_map(
        per_device,
        mesh=mesh,
        in_specs=(
            P(("groups", "pb"), None, None),
            P(),
            P(None, "pb", None),
            P(),
            P(("groups", "pb"), None, None),
        ),
        out_specs=P(("groups", "pb"), None, None),
        check_vma=False,
    )
```
